32 devices in a mesh: row: 2 (over x), col: 4 (over z), layer: 4 (over y, core).
Axes of the slice: x: 2, y: 2, z: 4, core: 2. Of those that a mesh axis runs over, the one named last changes fastest.
Arguments:
- a_blocks: float32 [2, 128, 128, 128], P('row', ('col', 'layer')), may hold values from -0.5 to 0.5
- b_blocks: float32 [32, 4, 128, 128], P(('row', 'layer'), 'col'), may hold values from -5 to 5
- pair_plan: int32 [2, 4, 4, 2, 4, 3, 16], P('row', 'col', 'layer'), may hold values from 0 to 127, as said below
- pair_counts: int32 [2, 4, 4, 2, 4], P('row', 'col', 'layer'), may hold values from 0 to 16, as said below
Outputs:
- next_blocks: float32 [2, 4, 128, 128, 128], P('row', 'col', 'layer')
The draws below stay inside these ranges and needn't reach their ends.
Inputs may be any that keep to these rules, and one draw needn't show every extreme that they name: `pair_plan`: field 0 names a block of a_blocks whose index divided by 8 (rounded down) is congruent to m modulo 4; field 1 lies in 0 to 3 and field 2 in 0 to 31; entries past the count obey the same ranges. `pair_counts`: some entry equals 16 in every draw.
All inputs are finite; a program needn't handle non-finite values.
Results may differ from the reference program's by a relative error of at most 0.0003.
Values sent between devices are 32-bit elements; how exact they have to be, the bound alone decides.
No kernel may reach another device: no remote copies, remote signals or barrier semaphores. Data moves between devices by JAX's collectives and lax.ppermute only.
A program may use at most 128 MiB of HBM per device.

```python
import jax
import jax.numpy as jnp
from jax import lax

BS = 128
ACAP = 8
BCAP = 4
PCAP = 16
CL = 32
N_ROW = 2
N_COL = 4
N_LAYER = 4


def draw_pair_plan(key, part):
    shape = (N_ROW, N_COL, N_LAYER, N_ROW, N_LAYER, PCAP)
    keys = jax.random.split(jax.random.fold_in(key, 11), 4)
    source_col = jax.random.randint(keys[0], shape, 0, N_COL)
    layer_ids = lax.broadcasted_iota(jnp.int32, shape, 4)
    within = jax.random.randint(keys[1], shape, 0, ACAP)
    left_ids = (source_col * N_LAYER + layer_ids) * ACAP + within
    right_ids = jax.random.randint(keys[2], shape, 0, BCAP)
    target = jax.random.randint(keys[3], shape, 0, CL)
    return jnp.stack([left_ids, right_ids, target], axis=5).astype(jnp.int32)


def draw_pair_counts(key, part):
    shape = (N_ROW, N_COL, N_LAYER, N_ROW, N_LAYER)
    keys = jax.random.split(jax.random.fold_in(key, 23), 3)
    level = jax.random.randint(keys[0], (N_ROW, N_COL, N_LAYER, 1, 1), 1, 5)
    upper = PCAP * level * level // 16
    lower = upper // 2
    spread = jax.random.randint(keys[1], shape, 0, PCAP + 1)
    counts = lower + spread % (upper - lower + 1)
    flat = counts.reshape(-1)
    chosen = jax.random.randint(keys[2], (), 0, flat.shape[0])
    flat = jnp.where(jnp.arange(flat.shape[0]) == chosen, PCAP, flat)
    return flat.reshape(shape).astype(jnp.int32)


def steps_of(rng, extent, cuts, low, largest):
    loudness = 1.0
    for position, parts in cuts:
        draws = jax.random.uniform(jax.random.fold_in(jax.random.fold_in(rng, 6), position), (parts,), jnp.float32, low / len(cuts), largest / len(cuts))
        loudness = loudness * jnp.repeat(jnp.exp(draws), extent[position] // parts).reshape((-1,) + (1,) * (len(extent) - 1 - position))
    return loudness


def gaussian(own_key, dims, scale, most, pieces=(), kind=jnp.bfloat16):
    drawn = jax.random.normal(own_key, dims, jnp.float32) * scale
    if len(pieces) > 0:
        drawn = steps_of(own_key, dims, pieces, -0.22, 0.18) * drawn
    return jnp.clip(drawn, min=-most, max=most).astype(kind)


def setup_inputs(seed: int = 0) -> dict:
    streams_of = jax.random.split(jax.random.key(seed), 5)
    return {
        "a_blocks": gaussian(streams_of[0], (N_ROW, N_COL * N_LAYER * ACAP, BS, BS), BS ** -0.5, 0.5, ((0, 2), (1, 16)), jnp.float32),
        "b_blocks": gaussian(streams_of[1], (N_ROW * N_LAYER * BCAP, N_COL, BS, BS), ((3 * CL / (N_ROW * N_LAYER * PCAP)) ** 0.5), 5.0, ((0, 8), (1, 4)), jnp.float32),
        "pair_plan": draw_pair_plan(jax.random.fold_in(streams_of[4], 71), 0),
        "pair_counts": draw_pair_counts(jax.random.fold_in(streams_of[4], 71), 0),
    }


def reference(a_blocks, b_blocks, pair_plan, pair_counts):
    devices = N_ROW * N_COL * N_LAYER
    sources = N_ROW * N_LAYER
    plans = pair_plan.reshape(devices, sources, 3, PCAP)
    counts = pair_counts.reshape(devices, sources)
    device_ids = jnp.arange(devices, dtype=jnp.int32)

    def one_device(item):
        ident, plan, count = item
        row_id = (ident // (N_COL * N_LAYER)).astype(jnp.int32)
        col_id = ((ident // N_LAYER) % N_COL).astype(jnp.int32)
        left_blocks = lax.dynamic_index_in_dim(a_blocks, row_id, 0, keepdims=False)
        right_blocks = lax.dynamic_index_in_dim(b_blocks, col_id, 1, keepdims=False)
        source_ids = jnp.arange(sources, dtype=jnp.int32)[:, None]
        left_ids = plan[:, 0, :].reshape(-1)
        right_ids = (plan[:, 1, :] + source_ids * BCAP).reshape(-1)
        target = plan[:, 2, :].reshape(-1)
        live = (jnp.arange(PCAP, dtype=jnp.int32)[None, :] < count[:, None]).reshape(-1)
        lhs = jnp.take(left_blocks, left_ids, axis=0)
        rhs = jnp.take(right_blocks, right_ids, axis=0)
        products = jnp.einsum("pij,pjk->pik", lhs, rhs, precision=lax.Precision.HIGHEST)
        products = jnp.where(live[:, None, None], products, jnp.zeros_like(products))
        return jax.ops.segment_sum(products, target, num_segments=CL)

    result = lax.map(one_device, (device_ids, plans, counts))
    return result.reshape(N_ROW, N_COL, N_LAYER * CL, BS, BS)
```

```python
import functools

import jax
import jax.numpy as jnp
from jax import lax
from jax.experimental import pallas as pl
from jax.experimental.pallas import tpu as pltpu
from jax.sharding import PartitionSpec as P

CL = 32
UNROLL = 8
F32 = jnp.float32
BF16 = jnp.bfloat16


def sort_kernel(rel_of, stage_of, base_of, a_cap, b_of, plan, counts, lists, sizes, stage_tab, base_tab):
    shards, layers, _, _ = plan.shape
    n_col = stage_tab.shape[0] // layers
    stages = sizes.shape[0]
    room = lists.shape[1]
    z, me = lax.axis_index("col"), lax.axis_index("layer")
    row = lax.axis_index("row")
    rels = sorted({rel for rel, _ in stage_of})
    for zp in range(n_col):
        rel = rel_of(zp, z)
        for dm in range(layers):
            stage = jnp.int32(0)
            base = jnp.int32(0)
            for r in rels:
                stage = jnp.where(rel == r, stage_of[r, dm], stage)
                base = jnp.where(rel == r, base_of[r, dm], base)
            stage_tab[zp * layers + dm] = stage
            base_tab[zp * layers + dm] = base
    for st in range(stages):
        sizes[st] = 0

    def per_list(q, _):
        s, m = q // layers, q % layers
        dm = m ^ me
        b_base = b_of(s, row, dm)

        def per_pair(p, _):
            left = plan[s, m, 0, p]
            at = (left // (layers * a_cap)) * layers + dm
            st = stage_tab[at]
            pos = sizes[st]
            lists[st, pos] = (
                (base_tab[at] + left % a_cap) | ((b_base + plan[s, m, 1, p]) << 10) | (plan[s, m, 2, p] << 20)
            )
            sizes[st] = pos + 1
            return 0

        return lax.fori_loop(0, counts[s, m], per_pair, 0)

    lax.fori_loop(0, shards * layers, per_list, 0)
    for st in range(stages):
        n = sizes[st]
        for u in range(UNROLL - 1):
            lists[st, n + u] = CL << 20
    del room


def halves(x):
    high = x.astype(BF16)
    return high, (x - high.astype(F32)).astype(BF16)


def product(a, b):
    ah, al = halves(a)
    bh, bl = halves(b)
    dot = functools.partial(jnp.dot, preferred_element_type=F32)
    return dot(ah, bh) + (dot(al, bh) + dot(ah, bl))


def stage_kernel(stage, a_at, n_a, n_b, carried, *refs):
    sizes, lists = refs[:2]
    a_refs = refs[2 : 2 + n_a]
    b_refs = refs[2 + n_a : 2 + n_a + n_b]
    rest = refs[2 + n_a + n_b :]
    if carried:
        acc_in, out, a_buf, b_buf, acc, sems = rest
    else:
        out, a_buf, b_buf, acc, sems = rest
    copies = []
    at = 0
    for ref in b_refs:
        n = ref.shape[0]
        copies.append(pltpu.make_async_copy(ref, b_buf.at[pl.ds(at, n)], sems.at[len(copies)]))
        at += n
    for ref, (at, n) in zip(a_refs, a_at):
        copies.append(pltpu.make_async_copy(ref.at[pl.ds(0, n)], a_buf.at[pl.ds(at, n)], sems.at[len(copies)]))
    if carried:
        copies.append(pltpu.make_async_copy(acc_in, acc.at[pl.ds(0, CL)], sems.at[len(copies)]))
    for copy in copies:
        copy.start()
    if carried:
        acc[CL] = jnp.zeros(acc.shape[1:], F32)
    else:
        acc[...] = jnp.zeros(acc.shape, F32)
    for copy in copies:
        copy.wait()

    def body(i, _):
        terms = []
        for u in range(UNROLL):
            entry = lists[stage, i * UNROLL + u]
            terms.append((entry >> 20, product(a_buf[entry & 1023], b_buf[(entry >> 10) & 1023])))
        for target, term in terms:
            acc[target] = acc[target] + term
        return 0

    lax.fori_loop(0, (sizes[stage] + UNROLL - 1) // UNROLL, body, 0)
    done = pltpu.make_async_copy(acc.at[pl.ds(0, CL)], out, sems.at[0])
    done.start()
    done.wait()


def run_stage(stage, sizes, lists, a_parts, b_parts, acc):
    bs = b_parts[0].shape[1:]
    n_blocks = max(at + n for _, at, n in a_parts)
    b_blocks = sum(b.shape[0] for b in b_parts)
    anywhere = pl.BlockSpec(memory_space=pl.ANY)
    smem = pl.BlockSpec(memory_space=pltpu.SMEM)
    arrays = [a for a, _, _ in a_parts] + list(b_parts) + ([] if acc is None else [acc])
    pairs = lists.shape[1] // 2
    return pl.pallas_call(
        functools.partial(
            stage_kernel, stage, [(at, n) for _, at, n in a_parts], len(a_parts), len(b_parts), acc is not None
        ),
        out_shape=jax.ShapeDtypeStruct((CL,) + bs, F32),
        in_specs=[smem, smem] + [anywhere] * len(arrays),
        out_specs=anywhere,
        scratch_shapes=[
            pltpu.VMEM((n_blocks,) + bs, F32),
            pltpu.VMEM((b_blocks,) + bs, F32),
            pltpu.VMEM((CL + 1,) + bs, F32),
            pltpu.SemaphoreType.DMA((len(arrays),)),
        ],
        cost_estimate=pl.CostEstimate(
            flops=6 * pairs * bs[0] * bs[0] * bs[1], bytes_accessed=4 * bs[0] * bs[1] * 80, transcendentals=0
        ),
        name=f"stage_{stage}",
    )(sizes, lists, *arrays)


def per_device(a_blocks, b_blocks, pair_plan, pair_counts):
    n_row, n_col, n_layer = (lax.axis_size(x) for x in ("row", "col", "layer"))
    z = lax.axis_index("col")
    own, b_own = a_blocks[0], b_blocks[:, 0]
    a_cap, b_cap = own.shape[0], b_own.shape[0]
    plan, counts = pair_plan[0, 0, 0], pair_counts[0, 0, 0]
    half = n_layer // 2

    def over_layer(x, d):
        return lax.ppermute(x, "layer", [(i, i ^ d) for i in range(n_layer)])

    def over_row(x):
        return lax.ppermute(x, "row", [(i, i ^ 1) for i in range(n_row)])

    def pairs_end(x):
        return lax.ppermute(x, "col", [(i, i ^ 1) for i in range(n_col)])

    def pairs_mid(x):
        moves = []
        for c in range(n_col):
            inner = 0 < c < n_col - 1
            for m in range(n_layer):
                to = (c - 1 if c % 2 == 0 else c + 1, m) if inner else (c, m ^ 1)
                moves.append((c * n_layer + m, to[0] * n_layer + to[1]))
        return lax.ppermute(x, ("col", "layer"), moves)

    is_end = jnp.logical_or(z == 0, z == n_col - 1)
    g = a_cap * 3 // 4
    y_own = over_layer(own, half)
    p_a = pairs_end(own)
    p_b = pairs_mid(own)
    y_b = over_layer(b_own, half)
    x_b = over_row(b_own)
    q = pairs_mid(p_a)
    r = pairs_end(p_b)
    y_a = over_layer(p_a[g:], half)
    x2 = jnp.where(is_end, r, p_b)
    y_2 = over_layer(x2, half)
    x_yb = over_row(y_b)
    t = pairs_end(q)
    x3 = jnp.where(is_end, t, q)
    y_3 = over_layer(x3, half)
    p_y = pairs_end(y_own[:g])

    stages = [
        [((0, 0), [own]), ((1, 0), [p_a]), ((0, half), [y_own])],
        [((2, 0), [x2]), ((3, 0), [x3]), ((1, half), [p_y, y_a]), ((2, half), [y_2])],
        [((3, half), [y_3])],
    ]
    stage_of, base_of, a_parts = {}, {}, []
    for st, groups in enumerate(stages):
        at, parts = 0, []
        for (rel, dm), arrays in groups:
            for other in (0, 1):
                stage_of[rel, dm ^ other], base_of[rel, dm ^ other] = st, at
                for x in arrays:
                    parts.append((over_layer(x, 1) if other else x, at, x.shape[0]))
                    at += x.shape[0]
        a_parts.append(parts)

    b_parts = []
    for x in (b_own, x_b, y_b, x_yb):
        b_parts += [x, over_layer(x, 1)]

    def b_of(s, row, dm):
        return ((dm // half) * 4 + (s ^ row) * 2 + dm % half) * b_cap

    def rel_of(zp, z):
        far = jnp.int32(3 if zp in (0, n_col - 1) else 2)
        return jnp.where(z == zp, 0, jnp.where(z == zp ^ 1, 1, far))

    shards, layers, _, p_cap = plan.shape
    room = shards * layers * p_cap + UNROLL
    smem = pl.BlockSpec(memory_space=pltpu.SMEM)
    lists, sizes = pl.pallas_call(
        functools.partial(sort_kernel, rel_of, stage_of, base_of, a_cap, b_of),
        out_shape=(
            jax.ShapeDtypeStruct((len(stages), room), jnp.int32),
            jax.ShapeDtypeStruct((len(stages),), jnp.int32),
        ),
        in_specs=[smem, smem],
        out_specs=(smem, smem),
        scratch_shapes=[pltpu.SMEM((n_col * layers,), jnp.int32), pltpu.SMEM((n_col * layers,), jnp.int32)],
        name="sort_pairs",
    )(plan, counts)
    acc = None
    for st, parts in enumerate(a_parts):
        acc = run_stage(st, sizes, lists, parts, b_parts, acc)
    return acc[None, None]


def solution(mesh):
    in_specs = (
        P("row", ("col", "layer"), None, None),
        P(("row", "layer"), "col", None, None),
        P("row", "col", "layer", None, None, None, None),
        P("row", "col", "layer", None, None),
    )
    out_specs = P("row", "col", "layer", None, None)
    return jax.shard_map(
        per_device, mesh=mesh, in_specs=in_specs, out_specs=out_specs, check_vma=False
    )
```

```python
import functools

import jax
import jax.numpy as jnp
from jax import lax
from jax.experimental import pallas as pl
from jax.experimental.pallas import tpu as pltpu
from jax.sharding import PartitionSpec as P


CL = 32
UNROLL = 8
VMEM_LIMIT = 20 << 20
F32 = jnp.float32
BF16 = jnp.bfloat16


def sort_kernel(rel_of, place_of, a_cap, cut, b_of, plan, counts, lists, sizes, stage_tab, base_tab):
    shards, layers, _, _ = plan.shape
    n_col = stage_tab.shape[0] // (2 * layers)
    stages = sizes.shape[0]
    z, me = lax.axis_index("col"), lax.axis_index("layer")
    row = lax.axis_index("row")
    rels = sorted({rel for rel, _, _ in place_of})
    for zp in range(n_col):
        rel = rel_of(zp, z)
        for dm in range(layers):
            for part in (0, 1):
                stage = jnp.int32(0)
                base = jnp.int32(0)
                for r in rels:
                    stage = jnp.where(rel == r, place_of[r, dm, part][0], stage)
                    base = jnp.where(rel == r, place_of[r, dm, part][1], base)
                stage_tab[(zp * layers + dm) * 2 + part] = stage
                base_tab[(zp * layers + dm) * 2 + part] = base
    for st in range(stages):
        sizes[st] = 0

    def per_list(q, _):
        s, m = q // layers, q % layers
        dm = m ^ me
        b_base = b_of(s, row, dm)

        def per_pair(p, _):
            left = plan[s, m, 0, p]
            within = left % a_cap
            at = ((left // (layers * a_cap)) * layers + dm) * 2 + jnp.where(within >= cut, 1, 0)
            st = stage_tab[at]
            pos = sizes[st]
            lists[st, pos] = (
                (base_tab[at] + within) | ((b_base + plan[s, m, 1, p]) << 10) | (plan[s, m, 2, p] << 20)
            )
            sizes[st] = pos + 1
            return 0

        return lax.fori_loop(0, counts[s, m], per_pair, 0)

    lax.fori_loop(0, shards * layers, per_list, 0)
    for st in range(stages):
        n = sizes[st]
        for u in range(UNROLL - 1):
            lists[st, n + u] = CL << 20


def halves(x):
    high = x.astype(BF16)
    return high, (x - high.astype(F32)).astype(BF16)


def product(a, b):
    ah, al = halves(a)
    bh, bl = halves(b)
    dot = functools.partial(jnp.dot, preferred_element_type=F32)
    return dot(ah, bh) + (dot(al, bh) + dot(ah, bl))


def stage_kernel(stage, a_at, n_a, n_b, carried, *refs):
    sizes, lists = refs[:2]
    a_refs = refs[2 : 2 + n_a]
    b_refs = refs[2 + n_a : 2 + n_a + n_b]
    rest = refs[2 + n_a + n_b :]
    if carried:
        acc_in, out, a_buf, b_buf, acc, sems = rest
    else:
        out, a_buf, b_buf, acc, sems = rest
    copies = []
    at = 0
    for ref in b_refs:
        n = ref.shape[0]
        copies.append(pltpu.make_async_copy(ref, b_buf.at[pl.ds(at, n)], sems.at[len(copies)]))
        at += n
    for ref, (at, n) in zip(a_refs, a_at):
        copies.append(pltpu.make_async_copy(ref.at[pl.ds(0, n)], a_buf.at[pl.ds(at, n)], sems.at[len(copies)]))
    if carried:
        copies.append(pltpu.make_async_copy(acc_in, acc.at[pl.ds(0, CL)], sems.at[len(copies)]))
    for copy in copies:
        copy.start()
    if carried:
        acc[CL] = jnp.zeros(acc.shape[1:], F32)
    else:
        acc[...] = jnp.zeros(acc.shape, F32)
    for copy in copies:
        copy.wait()

    def body(i, _):
        terms = []
        for u in range(UNROLL):
            entry = lists[stage, i * UNROLL + u]
            terms.append((entry >> 20, product(a_buf[entry & 1023], b_buf[(entry >> 10) & 1023])))
        for target, term in terms:
            acc[target] = acc[target] + term
        return 0

    lax.fori_loop(0, (sizes[stage] + UNROLL - 1) // UNROLL, body, 0)
    done = pltpu.make_async_copy(acc.at[pl.ds(0, CL)], out, sems.at[0])
    done.start()
    done.wait()


def run_stage(stage, sizes, lists, a_parts, b_parts, acc):
    bs = b_parts[0].shape[1:]
    n_blocks = max(at + n for _, at, n in a_parts)
    b_blocks = sum(b.shape[0] for b in b_parts)
    anywhere = pl.BlockSpec(memory_space=pl.ANY)
    smem = pl.BlockSpec(memory_space=pltpu.SMEM)
    arrays = [a for a, _, _ in a_parts] + list(b_parts) + ([] if acc is None else [acc])
    pairs = lists.shape[1] // 2
    return pl.pallas_call(
        functools.partial(
            stage_kernel, stage, [(at, n) for _, at, n in a_parts], len(a_parts), len(b_parts), acc is not None
        ),
        out_shape=jax.ShapeDtypeStruct((CL,) + bs, F32),
        in_specs=[smem, smem] + [anywhere] * len(arrays),
        out_specs=anywhere,
        scratch_shapes=[
            pltpu.VMEM((n_blocks,) + bs, F32),
            pltpu.VMEM((b_blocks,) + bs, F32),
            pltpu.VMEM((CL + 1,) + bs, F32),
            pltpu.SemaphoreType.DMA((len(arrays),)),
        ],
        cost_estimate=pl.CostEstimate(
            flops=6 * pairs * bs[0] * bs[0] * bs[1], bytes_accessed=4 * bs[0] * bs[1] * 80, transcendentals=0
        ),
        compiler_params=pltpu.CompilerParams(vmem_limit_bytes=VMEM_LIMIT),
    )(sizes, lists, *arrays)


def multiply(a_blocks, b_blocks, pair_plan, pair_counts):
    n_row, n_col, n_layer = (lax.axis_size(x) for x in ("row", "col", "layer"))
    z = lax.axis_index("col")
    own, b_own = a_blocks[0], b_blocks[:, 0]
    a_cap, b_cap = own.shape[0], b_own.shape[0]
    plan, counts = pair_plan[0, 0, 0], pair_counts[0, 0, 0]
    half = n_layer // 2

    def over_layer(x, d=half):
        return lax.ppermute(x, "layer", [(i, i ^ d) for i in range(n_layer)])

    def core(x):
        return over_layer(x, 1)

    def over_row(x):
        return lax.ppermute(x, "row", [(i, i ^ 1) for i in range(n_row)])

    def pairs_end(x):
        return lax.ppermute(x, "col", [(i, i ^ 1) for i in range(n_col)])

    def pairs_mid(x):
        moves = []
        for c in range(n_col):
            inner = 0 < c < n_col - 1
            for m in range(n_layer):
                to = (c - 1 if c % 2 == 0 else c + 1, m) if inner else (c, m ^ 1)
                moves.append((c * n_layer + m, to[0] * n_layer + to[1]))
        return lax.ppermute(x, ("col", "layer"), moves)

    is_end = jnp.logical_or(z == 0, z == n_col - 1)
    g = a_cap // 2
    y_own = over_layer(own)
    p_a = pairs_end(own)
    p_b = pairs_mid(own)
    swapped = n_row == 2
    b_here = b_own if swapped else lax.all_gather(b_own, "row", axis=0, tiled=True)
    y_b = over_layer(b_here)
    if swapped:
        x_b = over_row(b_own)
        b_rows = dict(b=b_own, xb=x_b, yb=y_b, xyb=over_row(y_b))
    else:
        b_rows = dict(b=b_here, yb=y_b)
    q = pairs_mid(p_a)
    r = pairs_end(p_b)
    y_a = over_layer(p_a[g:])
    x2 = jnp.where(is_end, r, p_b)
    y_2 = over_layer(x2)
    t = pairs_end(q)
    x3 = jnp.where(is_end, t, q)
    y_3 = over_layer(x3)
    p_y = pairs_end(y_own[:g])
    c_of = {}
    for name, x in dict(own=own, pa=p_a, yown=y_own, x2=x2, x3=x3, ya=y_a, y2=y_2, py=p_y, y3=y_3).items():
        c_of[name] = (x, core(x))

    stages = [
        [(0, 0, (0, 1), "own"), (1, 0, (0, 1), "pa"), (0, half, (0, 1), "yown")],
        [(2, 0, (0, 1), "x2"), (3, 0, (0, 1), "x3"), (1, half, (1,), "ya"), (2, half, (0, 1), "y2")],
        [(3, half, (0, 1), "y3"), (1, half, (0,), "py")],
    ]
    place_of, a_parts = {}, []
    for st, groups in enumerate(stages):
        at, parts = 0, []
        for rel, dm, halves_here, name in groups:
            for other in (0, 1):
                x = c_of[name][other]
                for part in halves_here:
                    place_of[rel, dm ^ other, part] = (st, at - (g if halves_here == (1,) else 0))
                parts.append((x, at, x.shape[0]))
                at += x.shape[0]
        a_parts.append(parts)

    b_parts = []
    for x in b_rows.values():
        b_parts += [x, core(x)]

    def b_of(s, row, dm):
        within = 0 if swapped else s * b_cap
        place = s ^ row if swapped else 0
        return ((dm // half) * len(b_rows) + place * 2 + dm % half) * b_parts[0].shape[0] + within

    def rel_of(zp, z):
        far = jnp.int32(3 if zp in (0, n_col - 1) else 2)
        return jnp.where(z == zp, 0, jnp.where(z == zp ^ 1, 1, far))

    shards, layers, _, p_cap = plan.shape
    room = shards * layers * p_cap + UNROLL
    smem = pl.BlockSpec(memory_space=pltpu.SMEM)
    lists, sizes = pl.pallas_call(
        functools.partial(sort_kernel, rel_of, place_of, a_cap, g, b_of),
        out_shape=(
            jax.ShapeDtypeStruct((len(stages), room), jnp.int32),
            jax.ShapeDtypeStruct((len(stages),), jnp.int32),
        ),
        in_specs=[smem, smem],
        out_specs=(smem, smem),
        scratch_shapes=[pltpu.SMEM((n_col * layers * 2,), jnp.int32)] * 2,
        cost_estimate=pl.CostEstimate(flops=0, bytes_accessed=4000, transcendentals=0),
        name="sort",
    )(plan, counts)
    acc = None
    for st, parts in enumerate(a_parts):
        acc = run_stage(st, sizes, lists, parts, b_parts, acc)
    return acc[None, None]


def solution(mesh):
    in_specs = (
        P("row", ("col", "layer"), None, None),
        P(("row", "layer"), "col", None, None),
        P("row", "col", "layer", None, None, None, None),
        P("row", "col", "layer", None, None),
    )
    out_specs = P("row", "col", "layer", None, None)
    return jax.shard_map(multiply, mesh=mesh, in_specs=in_specs, out_specs=out_specs, check_vma=False)
```

```python
import functools

import jax
import jax.numpy as jnp
from jax import lax
from jax.experimental import pallas as pl
from jax.experimental.pallas import tpu as pltpu
from jax.sharding import PartitionSpec as P


CL = 32
UNROLL = 8
VMEM_LIMIT = 20 << 20
F32 = jnp.float32
BF16 = jnp.bfloat16


def sort_kernel(rel_of, place_of, a_cap, cut, b_of, plan, counts, lists, sizes, stage_tab, base_tab):
    shards, _, layers, _ = plan.shape
    n_col = stage_tab.shape[0] // (2 * layers)
    stages = sizes.shape[0]
    z, me = lax.axis_index("col"), lax.axis_index("layer")
    row = lax.axis_index("row")
    rels = sorted({rel for rel, _, _ in place_of})
    for zp in range(n_col):
        rel = rel_of(zp, z)
        for dm in range(layers):
            for part in (0, 1):
                stage = jnp.int32(0)
                base = jnp.int32(0)
                for r in rels:
                    stage = jnp.where(rel == r, place_of[r, dm, part][0], stage)
                    base = jnp.where(rel == r, place_of[r, dm, part][1], base)
                stage_tab[(zp * layers + dm) * 2 + part] = stage
                base_tab[(zp * layers + dm) * 2 + part] = base
    for st in range(stages):
        sizes[st] = 0

    def per_list(q, _):
        s, m = q // layers, q % layers
        dm = m ^ me
        b_base = b_of(s, row, dm)

        def per_pair(p, _):
            left = plan[s, 0, m, p]
            within = left % a_cap
            at = ((left // (layers * a_cap)) * layers + dm) * 2 + jnp.where(within >= cut, 1, 0)
            st = stage_tab[at]
            pos = sizes[st]
            lists[st, pos] = (
                (base_tab[at] + within) | ((b_base + plan[s, 1, m, p]) << 10) | (plan[s, 2, m, p] << 20)
            )
            sizes[st] = pos + 1
            return 0

        return lax.fori_loop(0, counts[s, m], per_pair, 0)

    lax.fori_loop(0, shards * layers, per_list, 0)
    for st in range(stages):
        n = sizes[st]
        for u in range(UNROLL - 1):
            lists[st, n + u] = CL << 20


def halves(x):
    high = x.astype(BF16)
    return high, (x - high.astype(F32)).astype(BF16)


def product(a, b):
    ah, al = halves(a)
    bh, bl = halves(b)
    dot = functools.partial(jnp.dot, preferred_element_type=F32)
    return dot(ah, bh) + (dot(al, bh) + dot(ah, bl))


def stage_kernel(stage, a_at, n_a, n_b, carried, *refs):
    sizes, lists = refs[:2]
    a_refs = refs[2 : 2 + n_a]
    b_refs = refs[2 + n_a : 2 + n_a + n_b]
    rest = refs[2 + n_a + n_b :]
    if carried:
        acc_in, out, a_buf, b_buf, acc, sems = rest
    else:
        out, a_buf, b_buf, acc, sems = rest
    copies = []
    at = 0
    for ref in b_refs:
        n = ref.shape[0]
        copies.append(pltpu.make_async_copy(ref, b_buf.at[pl.ds(at, n)], sems.at[len(copies)]))
        at += n
    for ref, (at, n) in zip(a_refs, a_at):
        copies.append(pltpu.make_async_copy(ref.at[pl.ds(0, n)], a_buf.at[pl.ds(at, n)], sems.at[len(copies)]))
    if carried:
        copies.append(pltpu.make_async_copy(acc_in, acc.at[pl.ds(0, CL)], sems.at[len(copies)]))
    for copy in copies:
        copy.start()
    if carried:
        acc[CL] = jnp.zeros(acc.shape[1:], F32)
    else:
        acc[...] = jnp.zeros(acc.shape, F32)
    for copy in copies:
        copy.wait()

    def body(i, _):
        terms = []
        for u in range(UNROLL):
            entry = lists[stage, i * UNROLL + u]
            terms.append((entry >> 20, product(a_buf[entry & 1023], b_buf[(entry >> 10) & 1023])))
        for target, term in terms:
            acc[target] = acc[target] + term
        return 0

    lax.fori_loop(0, (sizes[stage] + UNROLL - 1) // UNROLL, body, 0)
    done = pltpu.make_async_copy(acc.at[pl.ds(0, CL)], out, sems.at[0])
    done.start()
    done.wait()


def run_stage(stage, sizes, lists, a_parts, b_parts, acc):
    bs = b_parts[0].shape[1:]
    n_blocks = max(at + n for _, at, n in a_parts)
    b_blocks = sum(b.shape[0] for b in b_parts)
    anywhere = pl.BlockSpec(memory_space=pl.ANY)
    smem = pl.BlockSpec(memory_space=pltpu.SMEM)
    arrays = [a for a, _, _ in a_parts] + list(b_parts) + ([] if acc is None else [acc])
    pairs = lists.shape[1] // 2
    return pl.pallas_call(
        functools.partial(
            stage_kernel, stage, [(at, n) for _, at, n in a_parts], len(a_parts), len(b_parts), acc is not None
        ),
        out_shape=jax.ShapeDtypeStruct((CL,) + bs, F32),
        in_specs=[smem, smem] + [anywhere] * len(arrays),
        out_specs=anywhere,
        scratch_shapes=[
            pltpu.VMEM((n_blocks,) + bs, F32),
            pltpu.VMEM((b_blocks,) + bs, F32),
            pltpu.VMEM((CL + 1,) + bs, F32),
            pltpu.SemaphoreType.DMA((len(arrays),)),
        ],
        cost_estimate=pl.CostEstimate(
            flops=6 * pairs * bs[0] * bs[0] * bs[1], bytes_accessed=4 * bs[0] * bs[1] * 80, transcendentals=0
        ),
        compiler_params=pltpu.CompilerParams(vmem_limit_bytes=VMEM_LIMIT),
    )(sizes, lists, *arrays)


def multiply(a_blocks, b_blocks, pair_plan, pair_counts):
    n_row, n_col, n_layer = (lax.axis_size(x) for x in ("row", "col", "layer"))
    z = lax.axis_index("col")
    own, b_own = a_blocks[0], b_blocks[:, 0]
    a_cap, b_cap = own.shape[0], b_own.shape[0]
    plan, counts = pair_plan[0, 0, 0], pair_counts[0, 0, 0]
    half = n_layer // 2

    def over_layer(x, d=half):
        return lax.ppermute(x, "layer", [(i, i ^ d) for i in range(n_layer)])

    def core(x):
        return over_layer(x, 1)

    def over_row(x):
        return lax.ppermute(x, "row", [(i, i ^ 1) for i in range(n_row)])

    def pairs_end(x):
        return lax.ppermute(x, "col", [(i, i ^ 1) for i in range(n_col)])

    def pairs_mid(x):
        moves = []
        for c in range(n_col):
            inner = 0 < c < n_col - 1
            for m in range(n_layer):
                to = (c - 1 if c % 2 == 0 else c + 1, m) if inner else (c, m ^ 1)
                moves.append((c * n_layer + m, to[0] * n_layer + to[1]))
        return lax.ppermute(x, ("col", "layer"), moves)

    is_end = jnp.logical_or(z == 0, z == n_col - 1)
    h = a_cap // 2
    g = a_cap * 3 // 4
    got = dict(own=own)

    def keep(name, x):
        got[name] = x
        return x

    y_own = keep("yown", over_layer(own))
    swapped = n_row == 2
    b_here = b_own if swapped else lax.all_gather(b_own, "row", axis=0, tiled=True)
    y_b = over_layer(b_here)
    if swapped:
        x_b = over_row(b_own)
        b_rows = dict(b=b_own, xb=x_b, yb=y_b, xyb=over_row(y_b))
    else:
        b_rows = dict(b=b_here, yb=y_b)
    for i, piece in (("1", own[:h]), ("2", own[h:])):
        p_a = keep("pa" + i, pairs_end(piece))
        p_b = pairs_mid(piece)
        q = pairs_mid(p_a)
        r = pairs_end(p_b)
        t = pairs_end(q)
        x2 = keep("x2" + i, jnp.where(is_end, r, p_b))
        x3 = keep("x3" + i, jnp.where(is_end, t, q))
        keep("y2" + i, over_layer(x2))
        keep("y3" + i, over_layer(x3))
    keep("ya", over_layer(got["pa2"][g - h :]))
    keep("py", pairs_end(y_own[:g]))
    c_of = {name: (x, core(x)) for name, x in got.items()}

    stages = [
        [(0, 0, (0, 1), ("own",)), (1, 0, (0, 1), ("pa1", "pa2")), (0, half, (0, 1), ("yown",))],
        [
            (2, 0, (0, 1), ("x21", "x22")),
            (3, 0, (0, 1), ("x31", "x32")),
            (1, half, (1,), ("ya",)),
            (2, half, (0, 1), ("y21", "y22")),
        ],
        [(3, half, (0, 1), ("y31", "y32")), (1, half, (0,), ("py",))],
    ]
    place_of, a_parts = {}, []
    for st, groups in enumerate(stages):
        at, parts = 0, []
        for rel, dm, which, names in groups:
            for other in (0, 1):
                for part in which:
                    place_of[rel, dm ^ other, part] = (st, at - (g if which == (1,) else 0))
                for name in names:
                    x = c_of[name][other]
                    parts.append((x, at, x.shape[0]))
                    at += x.shape[0]
        a_parts.append(parts)

    b_parts = []
    for x in b_rows.values():
        b_parts += [x, core(x)]

    def b_of(s, row, dm):
        within = 0 if swapped else s * b_cap
        place = s ^ row if swapped else 0
        return ((dm // half) * len(b_rows) + place * 2 + dm % half) * b_parts[0].shape[0] + within

    def rel_of(zp, z):
        far = jnp.int32(3 if zp in (0, n_col - 1) else 2)
        return jnp.where(z == zp, 0, jnp.where(z == zp ^ 1, 1, far))

    shards, layers, _, p_cap = plan.shape
    room = shards * layers * p_cap + UNROLL
    smem = pl.BlockSpec(memory_space=pltpu.SMEM)
    lists, sizes = pl.pallas_call(
        functools.partial(sort_kernel, rel_of, place_of, a_cap, g, b_of),
        out_shape=(
            jax.ShapeDtypeStruct((len(stages), room), jnp.int32),
            jax.ShapeDtypeStruct((len(stages),), jnp.int32),
        ),
        in_specs=[smem, smem],
        out_specs=(smem, smem),
        scratch_shapes=[pltpu.SMEM((n_col * layers * 2,), jnp.int32)] * 2,
        cost_estimate=pl.CostEstimate(flops=0, bytes_accessed=4000, transcendentals=0),
        name="sort",
    )(plan.transpose(0, 2, 1, 3), counts)
    acc = None
    for st, parts in enumerate(a_parts):
        acc = run_stage(st, sizes, lists, parts, b_parts, acc)
    return acc[None, None]


def solution(mesh):
    in_specs = (
        P("row", ("col", "layer"), None, None),
        P(("row", "layer"), "col", None, None),
        P("row", "col", "layer", None, None, None, None),
        P("row", "col", "layer", None, None),
    )
    out_specs = P("row", "col", "layer", None, None)
    return jax.shard_map(multiply, mesh=mesh, in_specs=in_specs, out_specs=out_specs, check_vma=False)
```
